256 devices in a mesh: gx: 16 (over x, z_hi), gy: 16 (over z_lo, y, core).
Axes of the slice: x: 4, y: 4, z: 8 (z_hi: 4, z_lo: 2; z = z_hi * 2 + z_lo), core: 2. Of those that a mesh axis runs over, the one named last changes fastest.
Arguments:
- tokens: bfloat16 [256, 256, 2, 512], P('gx', 'gy'), may hold values from -6 to 6
- cotangent: bfloat16 [256, 256, 2, 512], P('gx', 'gy'), may hold values from -6 to 6
- gain_x: float32 [512], replicated, may hold values from 0.1 to 1.9
- w_qkv_x: bfloat16 [512, 1536], replicated, may hold values from -5 to 5, as said below
- w_out_x: bfloat16 [512, 512], replicated, may hold values from -0.25 to 0.25
- gain_y: float32 [512], replicated, may hold values from 0.1 to 1.9
- w_qkv_y: bfloat16 [512, 1536], replicated, may hold values from -5 to 5, as said below
- w_out_y: bfloat16 [512, 512], replicated, may hold values from -0.25 to 0.25
- gain_mlp: float32 [512], replicated, may hold values from 0.1 to 1.9
- w_up: bfloat16 [512, 2048], replicated, may hold values from -0.25 to 0.25
- w_down: bfloat16 [2048, 512], replicated, may hold values from -0.125 to 0.125
Outputs:
- grad_tokens: bfloat16 [256, 256, 2, 512], P('gx', 'gy')
The draws below stay inside these ranges and needn't reach their ends.
Inputs may be any that keep to these rules, and one draw needn't show every extreme that they name: `w_qkv_x`: query, key and value projections side by side. `w_qkv_y`: query, key and value projections side by side.
All inputs are finite; a program needn't handle non-finite values.
Results may differ from the reference program's by a relative error of at most 0.013.
Values may be sent and summed in bfloat16 or wider, within the bound.
A program may use at most 128 MiB of HBM per device.

```python
from functools import partial
import jax
import jax.numpy as jnp
from jax import lax

D = 512
HEADS = 8
FF = 2048
DEPTH = 2
LX = 256
LY = 256


def qkv_weights(key, salt):
    base = jax.random.fold_in(key, salt)
    first = jax.random.fold_in(base, 0)
    second = jax.random.fold_in(base, 1)
    fourth = jax.random.fold_in(base, 3)
    scale = D ** (-0.5)
    query_cols = jnp.clip(jax.random.normal(first, (D, D), jnp.float32), -4.0, 4.0) * scale
    key_cols = jnp.clip(jax.random.normal(second, (D, D), jnp.float32), -4.0, 4.0) * scale
    value_cols = jnp.clip(jax.random.normal(fourth, (D, D), jnp.float32), -4.0, 4.0) * scale
    return jnp.concatenate([query_cols, key_cols, value_cols], 1).astype(jnp.bfloat16)


def draw_w_qkv_x(key, part):
    return qkv_weights(key, 11)


def draw_w_qkv_y(key, part):
    return qkv_weights(key, 12)


def block_levels(own_key, shape, pieces, least, top_value):
    def one(dim, parts):
        draws = jax.random.uniform(jax.random.fold_in(jax.random.fold_in(own_key, 6), dim), (parts,), jnp.float32, least / len(pieces), top_value / len(pieces))
        return jnp.repeat(jnp.exp(draws), shape[dim] // parts).reshape((-1,) + (1,) * (len(shape) - dim - 1))

    factor_of = one(*pieces[0])
    for cut in pieces[1:]:
        factor_of = factor_of * one(*cut)
    return factor_of


def normal_values(rng, extent, width, limit, cuts=(), held_as=jnp.bfloat16):
    values = width * jax.random.normal(rng, extent, jnp.float32)
    if cuts:
        values = values * block_levels(rng, extent, cuts, -0.22, 0.18)
    return jnp.clip(values, -limit, limit).astype(held_as)


def setup_inputs(seed: int = 0) -> dict:
    keys = jax.random.split(jax.random.key(seed), 12)
    tokens = normal_values(keys[0], (LX, LY, DEPTH, D), 1.0, 6.0, ((0, 16), (1, 16)))
    cotangent = normal_values(keys[1], (LX, LY, DEPTH, D), 1.0, 6.0, ((0, 16), (1, 16)))
    gain_x = jnp.clip(1.0 + 0.18 * jax.random.normal(keys[2], (D,), jnp.float32), 0.1, 1.9)
    w_qkv_x = draw_w_qkv_x(jax.random.fold_in(keys[11], 71), 0)
    w_out_x = normal_values(keys[4], (D, D), D ** -0.5, 0.25)
    gain_y = jnp.clip(1.0 + 0.18 * jax.random.normal(keys[5], (D,), jnp.float32), 0.1, 1.9)
    w_qkv_y = draw_w_qkv_y(jax.random.fold_in(keys[11], 71), 0)
    w_out_y = normal_values(keys[7], (D, D), D ** -0.5, 0.25)
    gain_mlp = jnp.clip(1.0 + 0.18 * jax.random.normal(keys[8], (D,), jnp.float32), 0.1, 1.9)
    w_up = normal_values(keys[9], (D, FF), D ** -0.5, 0.25)
    w_down = normal_values(keys[10], (FF, D), FF ** -0.5, 0.125)
    return dict(tokens=tokens, cotangent=cotangent, gain_x=gain_x, w_qkv_x=w_qkv_x, w_out_x=w_out_x, gain_y=gain_y, w_qkv_y=w_qkv_y, w_out_y=w_out_y, gain_mlp=gain_mlp, w_up=w_up, w_down=w_down)


def to_low(tensor):
    return lax.optimization_barrier(tensor.astype(jnp.bfloat16))

def layer_norm(inputs, norm_gain):
    average = lax.optimization_barrier(jnp.mean(inputs, -1, keepdims=True))
    centred = inputs - average
    variance = lax.optimization_barrier(jnp.mean(centred * centred, -1, keepdims=True))
    return centred * lax.rsqrt(variance + 1e-05) * norm_gain

def norm_back(inputs, norm_gain, gradient):
    _, pullback = jax.vjp(lambda tensor: layer_norm(tensor, norm_gain), inputs)
    return pullback(gradient)[0]

def project(tensor, weight):
    lead_dims = tensor.shape[:-1]
    flattened = tensor.reshape(-1, tensor.shape[-1])
    result = jnp.dot(flattened, weight, preferred_element_type=jnp.float32)
    return result.reshape(lead_dims + (weight.shape[1],))

def project_back(tensor, weight):
    lead_dims = tensor.shape[:-1]
    flattened = tensor.reshape(-1, tensor.shape[-1])
    result = lax.dot_general(flattened, weight, (((1,), (1,)), ((), ())), preferred_element_type=jnp.float32)
    return result.reshape(lead_dims + (weight.shape[0],))

def heads_of(tensor, which_part):
    lead_dims = tensor.shape[:-1]
    block_part = tensor[..., which_part * D:(which_part + 1) * D]
    return block_part.astype(jnp.float32).reshape(lead_dims + (HEADS, D // HEADS))

def softmax_rows(queries, key_part):
    scores = jnp.einsum('qzhd,kzhd->zhqk', queries, key_part) * (D // HEADS) ** (-0.5)
    highest = lax.optimization_barrier(jnp.max(scores, -1, keepdims=True))
    exponent = jnp.exp(scores - highest)
    return exponent / lax.optimization_barrier(jnp.sum(exponent, -1, keepdims=True))

def attend_slab(qkv_proj):
    queries, key_part, value_part = (heads_of(qkv_proj, 0), heads_of(qkv_proj, 1), heads_of(qkv_proj, 2))
    probs = softmax_rows(queries, key_part)
    probs_low = to_low(probs).astype(jnp.float32)
    result = jnp.einsum('zhqk,kzhd->qzhd', probs_low, value_part)
    return to_low(result.reshape(qkv_proj.shape[:-1] + (D,)))

def back_slab(qkv_proj, grad_out):
    queries, key_part, value_part = (heads_of(qkv_proj, 0), heads_of(qkv_proj, 1), heads_of(qkv_proj, 2))
    scale = (D // HEADS) ** (-0.5)
    probs = softmax_rows(queries, key_part)
    probs_low = to_low(probs).astype(jnp.float32)
    grad_heads = heads_of(grad_out, 0)
    grad_probs = jnp.einsum('qzhd,kzhd->zhqk', grad_heads, value_part)
    grad_scores = probs * (grad_probs - lax.optimization_barrier(jnp.sum(probs * grad_probs, -1, keepdims=True)))
    grad_low = to_low(grad_scores).astype(jnp.float32)
    grad_q = to_low(jnp.einsum('zhqk,kzhd->qzhd', grad_low, key_part) * scale)
    grad_k = to_low(jnp.einsum('zhqk,qzhd->kzhd', grad_low, queries) * scale)
    grad_v = to_low(jnp.einsum('zhqk,qzhd->kzhd', probs_low, grad_heads))
    lead_dims = qkv_proj.shape[:-1] + (D,)
    return jnp.concatenate([grad_q.reshape(lead_dims), grad_k.reshape(lead_dims), grad_v.reshape(lead_dims)], -1)

def along_x(action, *arrays):
    moved = tuple((jnp.moveaxis(member, 1, 0) for member in arrays))
    result = lax.map(lambda slabs: action(*slabs), moved)
    return jnp.moveaxis(result, 0, 1)

def along_y(action, *arrays):
    return lax.map(lambda slabs: action(*slabs), tuple(arrays))

def reference(tokens, cotangent, gain_x, w_qkv_x, w_out_x, gain_y, w_qkv_y, w_out_y, gain_mlp, w_up, w_down):
    stream_0 = tokens.astype(jnp.float32)
    qkv_x = to_low(project(to_low(layer_norm(stream_0, gain_x)), w_qkv_x))
    mixed_x = along_x(attend_slab, qkv_x)
    stream_1 = to_low(stream_0 + project(mixed_x, w_out_x))
    stream_1f = stream_1.astype(jnp.float32)
    qkv_y = to_low(project(to_low(layer_norm(stream_1f, gain_y)), w_qkv_y))
    mixed_y = along_y(attend_slab, qkv_y)
    stream_2 = to_low(stream_1f + project(mixed_y, w_out_y))
    stream_2f = stream_2.astype(jnp.float32)
    pre_act = project(to_low(layer_norm(stream_2f, gain_mlp)), w_up)
    grad_act = to_low(project_back(cotangent, w_down))
    _, pullback = jax.vjp(partial(jax.nn.gelu, approximate=True), pre_act)
    grad_pre = to_low(pullback(grad_act.astype(jnp.float32))[0])
    grad_2 = to_low(cotangent.astype(jnp.float32) + norm_back(stream_2f, gain_mlp, project_back(grad_pre, w_up)))
    grad_mixed_y = to_low(project_back(grad_2, w_out_y))
    grad_qkv_y = along_y(back_slab, qkv_y, grad_mixed_y)
    grad_1 = to_low(grad_2.astype(jnp.float32) + norm_back(stream_1f, gain_y, project_back(grad_qkv_y, w_qkv_y)))
    grad_mixed_x = to_low(project_back(grad_1, w_out_x))
    grad_qkv_x = along_x(back_slab, qkv_x, grad_mixed_x)
    grad_tokens = to_low(grad_1.astype(jnp.float32) + norm_back(stream_0, gain_x, project_back(grad_qkv_x, w_qkv_x)))
    return grad_tokens
```

```python
from functools import partial

import jax
import jax.numpy as jnp
from jax import lax
from jax.sharding import PartitionSpec as P

D = 512
HEADS = 8


def to_low(tensor):
    return lax.optimization_barrier(tensor.astype(jnp.bfloat16))


def layer_norm(inputs, norm_gain):
    average = jnp.mean(inputs, -1, keepdims=True)
    centred = inputs - average
    variance = jnp.mean(centred * centred, -1, keepdims=True)
    return centred * lax.rsqrt(variance + 1e-05) * norm_gain


def norm_back(inputs, norm_gain, gradient):
    _, pullback = jax.vjp(lambda tensor: layer_norm(tensor, norm_gain), inputs)
    return pullback(gradient)[0]


def project(tensor, weight):
    lead_dims = tensor.shape[:-1]
    flattened = tensor.reshape(-1, tensor.shape[-1])
    result = jnp.dot(flattened, weight, preferred_element_type=jnp.float32)
    return result.reshape(lead_dims + (weight.shape[1],))


def project_back(tensor, weight):
    lead_dims = tensor.shape[:-1]
    flattened = tensor.reshape(-1, tensor.shape[-1])
    result = lax.dot_general(
        flattened, weight, (((1,), (1,)), ((), ())), preferred_element_type=jnp.float32
    )
    return result.reshape(lead_dims + (weight.shape[0],))


def to_xlines(tensor):
    return lax.all_to_all(tensor, "gx", split_axis=1, concat_axis=0, tiled=True)


def from_xlines(tensor):
    return lax.all_to_all(tensor, "gx", split_axis=0, concat_axis=1, tiled=True)


def to_ylines(tensor):
    return lax.all_to_all(tensor, "gy", split_axis=0, concat_axis=1, tiled=True)


def from_ylines(tensor):
    return lax.all_to_all(tensor, "gy", split_axis=1, concat_axis=0, tiled=True)


def heads_of(tensor, which_part):
    lead_dims = tensor.shape[:-1]
    block_part = tensor[..., which_part * D : (which_part + 1) * D]
    return block_part.reshape(lead_dims + (HEADS, D // HEADS))


def softmax_rows(queries, key_part, layout, key_layout):
    scores = jnp.einsum(
        layout + "hd," + key_layout + "hd->bzhqk",
        queries,
        key_part,
        preferred_element_type=jnp.float32,
    )
    scores = scores * (D // HEADS) ** (-0.5)
    highest = jnp.max(scores, -1, keepdims=True)
    exponent = jnp.exp(scores - highest)
    return exponent / jnp.sum(exponent, -1, keepdims=True)


def attend(qkv_proj, layout):
    key_layout = layout.replace("q", "k")
    queries, key_part, value_part = (
        heads_of(qkv_proj, 0),
        heads_of(qkv_proj, 1),
        heads_of(qkv_proj, 2),
    )
    probs_low = softmax_rows(queries, key_part, layout, key_layout).astype(jnp.bfloat16)
    result = jnp.einsum(
        "bzhqk," + key_layout + "hd->" + layout + "hd",
        probs_low,
        value_part,
        preferred_element_type=jnp.float32,
    )
    return result.reshape(qkv_proj.shape[:-1] + (D,)).astype(jnp.bfloat16)


def attend_back(qkv_proj, grad_out, layout):
    key_layout = layout.replace("q", "k")
    scale = (D // HEADS) ** (-0.5)
    queries, key_part, value_part = (
        heads_of(qkv_proj, 0),
        heads_of(qkv_proj, 1),
        heads_of(qkv_proj, 2),
    )
    probs = softmax_rows(queries, key_part, layout, key_layout)
    probs_low = probs.astype(jnp.bfloat16)
    grad_heads = heads_of(grad_out, 0)
    grad_probs = jnp.einsum(
        layout + "hd," + key_layout + "hd->bzhqk",
        grad_heads,
        value_part,
        preferred_element_type=jnp.float32,
    )
    grad_scores = probs * (grad_probs - jnp.sum(probs * grad_probs, -1, keepdims=True))
    grad_low = grad_scores.astype(jnp.bfloat16)
    grad_q = jnp.einsum(
        "bzhqk," + key_layout + "hd->" + layout + "hd",
        grad_low,
        key_part,
        preferred_element_type=jnp.float32,
    )
    grad_k = jnp.einsum(
        "bzhqk," + layout + "hd->" + key_layout + "hd",
        grad_low,
        queries,
        preferred_element_type=jnp.float32,
    )
    grad_v = jnp.einsum(
        "bzhqk," + layout + "hd->" + key_layout + "hd",
        probs_low,
        grad_heads,
        preferred_element_type=jnp.float32,
    )
    lead_dims = qkv_proj.shape[:-1] + (D,)
    return jnp.concatenate(
        [
            (grad_q * scale).astype(jnp.bfloat16).reshape(lead_dims),
            (grad_k * scale).astype(jnp.bfloat16).reshape(lead_dims),
            grad_v.astype(jnp.bfloat16).reshape(lead_dims),
        ],
        -1,
    )


def mix_lines(stream, norm_gain, w_qkv, w_out, layout):
    stream_f = stream.astype(jnp.float32)
    normed = layer_norm(stream_f, norm_gain).astype(jnp.bfloat16)
    qkv_lines = project(normed, w_qkv).astype(jnp.bfloat16)
    mixed_out = attend(qkv_lines, layout)
    updated = to_low(stream_f + project(mixed_out, w_out))
    return (updated, qkv_lines)


def back_lines(stream, gradient, qkv_lines, norm_gain, w_qkv, w_out, layout):
    grad_mixed = project_back(gradient, w_out).astype(jnp.bfloat16)
    grad_qkv = attend_back(qkv_lines, grad_mixed, layout)
    grad_normed = project_back(grad_qkv, w_qkv)
    return to_low(
        gradient.astype(jnp.float32) + norm_back(stream.astype(jnp.float32), norm_gain, grad_normed)
    )


def mlp_back(stream, cotangent, gain_mlp, w_up, w_down):
    stream_f = stream.astype(jnp.float32)
    normed = layer_norm(stream_f, gain_mlp).astype(jnp.bfloat16)
    pre_act = project(normed, w_up)
    grad_act = project_back(cotangent, w_down).astype(jnp.bfloat16)
    _, pullback = jax.vjp(partial(jax.nn.gelu, approximate=True), pre_act)
    grad_pre = pullback(grad_act.astype(jnp.float32))[0].astype(jnp.bfloat16)
    return to_low(
        cotangent.astype(jnp.float32) + norm_back(stream_f, gain_mlp, project_back(grad_pre, w_up))
    )


def local(
    tokens, cotangent, gain_x, w_qkv_x, w_out_x, gain_y, w_qkv_y, w_out_y, gain_mlp, w_up, w_down
):
    tokens_x = to_xlines(tokens)
    cotangent_y = to_ylines(cotangent)
    stream_1x, qkv_x = mix_lines(tokens_x, gain_x, w_qkv_x, w_out_x, "qbz")
    stream_1 = to_ylines(from_xlines(stream_1x))
    stream_2, qkv_y = mix_lines(stream_1, gain_y, w_qkv_y, w_out_y, "bqz")
    grad_2 = mlp_back(stream_2, cotangent_y, gain_mlp, w_up, w_down)
    grad_1y = back_lines(stream_1, grad_2, qkv_y, gain_y, w_qkv_y, w_out_y, "bqz")
    grad_1 = to_xlines(from_ylines(grad_1y))
    grad_x = back_lines(tokens_x, grad_1, qkv_x, gain_x, w_qkv_x, w_out_x, "qbz")
    return from_xlines(grad_x)


def solution(mesh):
    in_specs = (
        P("gx", "gy", None, None),
        P("gx", "gy", None, None),
        P(),
        P(),
        P(),
        P(),
        P(),
        P(),
        P(),
        P(),
        P(),
    )
    out_specs = P("gx", "gy", None, None)
    return jax.shard_map(local, mesh=mesh, in_specs=in_specs, out_specs=out_specs, check_vma=False)
```

```python
import jax
import jax.numpy as jnp
from jax import lax
from jax.experimental import pallas as pl
from jax.experimental.pallas import tpu as pltpu
from jax.sharding import PartitionSpec as P

D = 512
HEADS = 8
HD = 64
FF = 2048
N = 256
MESH = pl.DeviceIdType.MESH
BF = jnp.bfloat16
F32 = jnp.float32

TOK, COT, Z2, XY2, XY3, Z3, OUT = 0, 2, 4, 6, 8, 10, 12
N_EX = 14


def nn(a, b):
    return jnp.dot(a, b, preferred_element_type=F32)


def nt(a, b):
    return lax.dot_general(a, b, (((1,), (1,)), ((), ())), preferred_element_type=F32)


def tn(a, b):
    return lax.dot_general(a, b, (((0,), (0,)), ((), ())), preferred_element_type=F32)


def norm_parts(v):
    c = v - jnp.mean(v, 0, keepdims=True)
    r = lax.rsqrt(jnp.mean(c * c, 0, keepdims=True) + 1e-05)
    return c * r, r


def norm_back(v, gain, e):
    xhat, r = norm_parts(v)
    dy = e * gain
    m1 = jnp.mean(dy, 0, keepdims=True)
    m2 = jnp.mean(dy * xhat, 0, keepdims=True)
    return r * (dy - m1 - xhat * m2)


def gelu_slope(x):
    k = 0.7978845608028654
    x2 = x * x
    t = jnp.tanh(k * x * (1.0 + 0.044715 * x2))
    return 0.5 * (1.0 + t) + (0.5 * k) * x * (1.0 - t * t) * (1.0 + 0.134145 * x2)


def kernel(
    tok, cot, gain_x, wqx, wox, gain_y, wqy, woy, gain_m, wup, wdn,
    out,
    wqx_v, wox_v, wqy_v, woy_v, wup_v, wdn_v,
    wqx_t, wox_t, wqy_t, woy_t, wup_t,
    gx_t, gy_t, gm_t, perm_a, perm_b, perm_c,
    xl, cl, s1x, zb, pb, yl, g1y, qb, rb, g1x, gtx,
    xt, s1t, s2t, g2t, ct, qkvx, qkvy, mix, nrm, gmx, gqkv, gpre, px, py,
    wsem, ssem, rsem,
):
    gx = lax.axis_index("gx")
    gy = lax.axis_index("gy")
    X, zh = gx // 4, gx % 4
    zl, Yc = gy // 8, gy % 8
    z = zh * 2 + zl
    d_me = X * 8 + Yc

    def at_z(zz):
        return (X * 4 + zz // 2, (zz % 2) * 8 + Yc)

    def at_d(d):
        return ((d // 8) * 4 + zh, zl * 8 + d % 8)

    def gx_peer(p):
        return lax.rem(gx + p, 16)

    def gy_peer(p):
        return lax.rem(gy + p, 16)

    def z_peer(p):
        return lax.rem(z + p, 8)

    def d_peer(p):
        return lax.rem(d_me + p, 32)

    barrier = pltpu.get_barrier_semaphore()

    def loop(lo, hi, body):
        def step(i, carry):
            body(i)
            return carry

        lax.fori_loop(lo, hi, step, 0)

    def greet(device):
        pl.semaphore_signal(barrier, inc=1, device_id=device, device_id_type=MESH)

    loop(1, 16, lambda p: greet((gx_peer(p), gy)))
    loop(1, 16, lambda p: greet((gx, gy_peer(p))))
    loop(1, 8, lambda p: greet(at_z(z_peer(p))))
    loop(1, 32, lambda p: greet(at_d(d_peer(p))))

    weights = (
        (wqx, wqx_v), (wox, wox_v), (wqy, wqy_v), (woy, woy_v), (wup, wup_v), (wdn, wdn_v)
    )
    loads = [pltpu.make_async_copy(s, d, wsem.at[i]) for i, (s, d) in enumerate(weights)]
    for load in loads:
        load.start()

    pl.semaphore_wait(barrier, 68)

    def put(src, dst, device, k):
        pltpu.make_async_remote_copy(
            src_ref=src, dst_ref=dst, send_sem=ssem.at[k], recv_sem=rsem.at[k],
            device_id=device, device_id_type=MESH,
        ).start()

    def keep(src, dst, k):
        pltpu.make_async_copy(src, dst, rsem.at[k]).start()

    def arrived(k):
        pltpu.make_async_copy(pb.at[0], pb.at[0], rsem.at[k]).wait()

    def sent(k, slabs):
        part = pb.at[0, pl.ds(0, slabs)]
        pltpu.make_async_copy(part, part, ssem.at[k]).wait()

    def send_tok(c):
        dst = xl.at[c, pl.ds(2 * zh, 2), X]
        keep(tok.at[gx, c], dst, TOK + c)

        def body(p):
            q = gx_peer(p)
            put(tok.at[q, c], dst, (q, gy), TOK + c)

        loop(1, 16, body)

    def send_cot(c):
        dst = cl.at[c, gy]
        keep(cot.at[gy, c], dst, COT + c)

        def body(p):
            q = gy_peer(p)
            put(cot.at[q, c], dst, (gx, q), COT + c)

        loop(1, 16, body)

    def send_z(src, dst, c, k):
        keep(src.at[c, z], dst.at[c, z], k + c)

        def body(p):
            q = z_peer(p)
            put(src.at[c, q], dst.at[c, z], at_z(q), k + c)

        loop(1, 8, body)

    def send_d(src, dst, c, k):
        keep(src.at[c, d_me], dst.at[c, d_me], k + c)

        def body(p):
            q = d_peer(p)
            put(src.at[c, q], dst.at[c, d_me], at_d(q), k + c)

        loop(1, 32, body)

    def send_out(c):
        dst = out.at[gx, c]
        keep(gtx.at[c, pl.ds(2 * zh, 2), X], dst, OUT + c)

        def body(p):
            q = gx_peer(p)
            put(gtx.at[c, pl.ds(2 * (q % 4), 2), q // 4], dst, (q, gy), OUT + c)

        loop(1, 16, body)

    send_tok(0)
    send_tok(1)

    for g, gt in ((gain_x, gx_t), (gain_y, gy_t), (gain_m, gm_t)):
        col = jnp.transpose(jnp.broadcast_to(g[...], (128, D)))
        gt[:, :128] = col
        gt[:, 128:] = col
    row = lax.broadcasted_iota(jnp.int32, (N, N), 0)
    colm = lax.broadcasted_iota(jnp.int32, (N, N), 1)
    perm_a[...] = jnp.where(colm == (row % 8) * 32 + row // 8, 1.0, 0.0).astype(BF)
    perm_b[...] = jnp.where(colm == (row % 32) * 8 + row // 32, 1.0, 0.0).astype(BF)
    rX, rY, rh, rl = row // 64, (row // 8) % 8, (row // 2) % 4, row % 2
    perm_c[...] = jnp.where(colm == (rl * 8 + rY) * 16 + rX * 4 + rh, 1.0, 0.0).astype(BF)

    def flip(src, dst, cols):
        def body(i):
            s = pl.multiple_of(i * 256, 256)
            dst[pl.ds(s, 256), :] = jnp.transpose(src[:, pl.ds(s, 256)])

        loop(0, cols // 256, body)

    loads[0].wait()
    flip(wqx_v, wqx_t, 1536)
    loads[1].wait()
    flip(wox_v, wox_t, D)
    loads[2].wait()
    flip(wqy_v, wqy_t, 1536)
    loads[3].wait()
    flip(woy_v, woy_t, D)
    loads[4].wait()
    flip(wup_v, wup_t, FF)
    loads[5].wait()

    def blocks(rows, body, size=256):
        loop(0, rows // size, lambda i: body(pl.ds(pl.multiple_of(i * size, size), size)))

    def forward(src_t, gain_t, wq_t, wo_t, qkv, probs, dst_t):
        xhat, _ = norm_parts(src_t[...].astype(F32))
        nrm[...] = (xhat * gain_t[...]).astype(BF)

        def proj(s):
            qkv[s, :] = nn(wq_t[s, :], nrm[...]).astype(BF)

        blocks(1536, proj)

        def head(h):
            o = pl.multiple_of(h * HD, HD)
            q = qkv[pl.ds(o, HD), :] * 0.125
            k = qkv[pl.ds(o + D, HD), :]
            v = qkv[pl.ds(o + 2 * D, HD), :]
            s = tn(k, q)
            e = jnp.exp(s - jnp.max(s, 0, keepdims=True))
            p = e * (1.0 / jnp.sum(e, 0, keepdims=True))
            probs[h] = p
            mix[pl.ds(o, HD), :] = nn(v, p.astype(BF)).astype(BF)

        loop(0, HEADS, head)

        def fin(s):
            dst_t[s, :] = (src_t[s, :].astype(F32) + nn(wo_t[s, :], mix[...])).astype(BF)

        blocks(D, fin)

    def heads_back(qkv, probs, grad_t, wo):
        def gm(s):
            gmx[s, :] = nn(wo[s, :], grad_t[...]).astype(BF)

        blocks(D, gm)

        def head(h):
            o = pl.multiple_of(h * HD, HD)
            q = qkv[pl.ds(o, HD), :]
            k = qkv[pl.ds(o + D, HD), :]
            v = qkv[pl.ds(o + 2 * D, HD), :]
            g = gmx[pl.ds(o, HD), :]
            p = probs[h]
            dp = tn(v, g)
            ds = (p * (dp - jnp.sum(p * dp, 0, keepdims=True))).astype(BF)
            gqkv[pl.ds(o, HD), :] = (nn(k, ds) * 0.125).astype(BF)
            gqkv[pl.ds(o + D, HD), :] = (nt(q, ds) * 0.125).astype(BF)
            gqkv[pl.ds(o + 2 * D, HD), :] = nt(g, p.astype(BF)).astype(BF)

        loop(0, HEADS, head)

    def finish_back(src_t, grad_t, gain_t, wq):
        e = nn(wq[...], gqkv[...])
        return grad_t[...].astype(F32) + norm_back(src_t[...].astype(F32), gain_t[...], e)

    def rows(buf):
        return buf[...].reshape(N, D)

    def x_fwd(c):
        arrived(TOK + c)
        xt[c] = jnp.transpose(rows(xl.at[c]))
        forward(xt.at[c], gx_t, wqx_t, wox_t, qkvx.at[c], px.at[c], s2t)
        s1x[c] = jnp.transpose(s2t[...]).reshape(8, 32, D)
        send_z(s1x, zb, c, Z2)

    def relay2(c):
        arrived(Z2 + c)
        pb[c] = nn(perm_a[...], rows(zb.at[c])).astype(BF).reshape(32, 8, D)
        send_d(pb, yl, c, XY2)

    def relay3(c):
        arrived(XY3 + c)
        rb[c] = nn(perm_b[...], rows(qb.at[c])).astype(BF).reshape(8, 32, D)
        send_z(rb, g1x, c, Z3)

    def y_fwd(c):
        arrived(XY2 + c)
        s1t[...] = jnp.transpose(rows(yl.at[c]))
        forward(s1t, gy_t, wqy_t, woy_t, qkvy, py, s2t)

    def y_mlp(c):
        arrived(COT + c)
        ct[...] = jnp.transpose(nn(perm_c[...], rows(cl.at[c])).astype(BF))
        xhat, _ = norm_parts(s2t[...].astype(F32))
        nrm[...] = (xhat * gm_t[...]).astype(BF)

        def hidden(s):
            act = nn(wup_t[s, :], nrm[...])
            grad = nn(wdn_v[s, :], ct[...]).astype(BF).astype(F32)
            gpre[s, :] = (grad * gelu_slope(act)).astype(BF)

        blocks(FF, hidden)
        e = nn(wup_v[...], gpre[...])
        g2t[...] = (
            ct[...].astype(F32) + norm_back(s2t[...].astype(F32), gm_t[...], e)
        ).astype(BF)

    def y_bwd(c):
        heads_back(qkvy, py, g2t, woy_v)
        g = finish_back(s1t, g2t, gy_t, wqy_v).astype(BF)
        g1y[c] = jnp.transpose(g).reshape(32, 8, D)
        send_d(g1y, qb, c, XY3)

    def x_bwd(c, between):
        arrived(Z3 + c)
        g2t[...] = jnp.transpose(rows(g1x.at[c]))
        heads_back(qkvx.at[c], px.at[c], g2t, wox_v)
        between()
        g = finish_back(xt.at[c], g2t, gx_t, wqx_v).astype(BF)
        gtx[c] = jnp.transpose(g).reshape(8, 4, 8, D)
        send_out(c)

    x_fwd(0)
    send_cot(0)
    send_cot(1)
    x_fwd(1)
    relay2(0)
    y_fwd(0)
    relay2(1)
    y_mlp(0)
    y_bwd(0)
    y_fwd(1)
    relay3(0)
    y_mlp(1)
    y_bwd(1)
    x_bwd(0, lambda: relay3(1))
    x_bwd(1, lambda: None)

    for c in range(2):
        arrived(OUT + c)
        sent(TOK + c, 30)
        sent(COT + c, 30)
        sent(Z2 + c, 28)
        sent(XY2 + c, 31)
        sent(XY3 + c, 31)
        sent(Z3 + c, 28)
        sent(OUT + c, 30)


def local(
    tokens, cotangent, gain_x, w_qkv_x, w_out_x, gain_y, w_qkv_y, w_out_y, gain_mlp, w_up, w_down
):
    tok = jnp.transpose(tokens, (1, 2, 0, 3)).reshape(16, 2, 2, 8, D)
    cot = jnp.transpose(cotangent, (0, 2, 1, 3))
    any_spec = pl.BlockSpec(memory_space=pl.ANY)
    vm = pl.BlockSpec(memory_space=pltpu.VMEM)
    V = pltpu.VMEM
    scratch = [
        V((D, 1536), BF), V((D, D), BF), V((D, 1536), BF), V((D, D), BF), V((D, FF), BF),
        V((FF, D), BF),
        V((1536, D), BF), V((D, D), BF), V((1536, D), BF), V((D, D), BF), V((FF, D), BF),
        V((D, N), F32), V((D, N), F32), V((D, N), F32),
        V((N, N), BF), V((N, N), BF), V((N, N), BF),
        V((2, 8, 4, 8, D), BF),
        V((2, 16, 16, D), BF),
        V((2, 8, 32, D), BF),
        V((2, 8, 32, D), BF),
        V((2, 32, 8, D), BF),
        V((2, 32, 8, D), BF),
        V((2, 32, 8, D), BF),
        V((2, 32, 8, D), BF),
        V((2, 8, 32, D), BF),
        V((2, 8, 32, D), BF),
        V((2, 8, 4, 8, D), BF),
        V((2, D, N), BF),
        V((D, N), BF), V((D, N), BF), V((D, N), BF), V((D, N), BF),
        V((2, 1536, N), BF), V((1536, N), BF),
        V((D, N), BF), V((D, N), BF), V((D, N), BF),
        V((1536, N), BF), V((FF, N), BF),
        V((2, HEADS, N, N), F32), V((HEADS, N, N), F32),
        pltpu.SemaphoreType.DMA((6,)),
        pltpu.SemaphoreType.DMA((N_EX,)),
        pltpu.SemaphoreType.DMA((N_EX,)),
    ]
    res = pl.pallas_call(
        kernel,
        out_shape=jax.ShapeDtypeStruct((16, 2, 2, 8, D), BF),
        in_specs=[any_spec, any_spec, vm, any_spec, any_spec, vm, any_spec, any_spec, vm,
                  any_spec, any_spec],
        out_specs=any_spec,
        scratch_shapes=scratch,
        compiler_params=pltpu.CompilerParams(
            collective_id=0, has_side_effects=True, vmem_limit_bytes=60 * 1024 * 1024
        ),
        name="axial_grad",
    )(
        tok, cot, gain_x.reshape(1, D), w_qkv_x, w_out_x, gain_y.reshape(1, D), w_qkv_y, w_out_y,
        gain_mlp.reshape(1, D), w_up, w_down,
    )
    return jnp.transpose(res.reshape(16, 2, 16, D), (2, 0, 1, 3))


def solution(mesh):
    in_specs = (P("gx", "gy", None, None), P("gx", "gy", None, None)) + (P(),) * 9
    out_specs = P("gx", "gy", None, None)
    return jax.shard_map(local, mesh=mesh, in_specs=in_specs, out_specs=out_specs, check_vma=False)
```

```python
import jax
import jax.numpy as jnp
from jax import lax
from jax.experimental import pallas as pl
from jax.experimental.pallas import tpu as pltpu
from jax.sharding import PartitionSpec as P

D = 512
HEADS = 8
HD = 64
FF = 2048
N = 256
MESH = pl.DeviceIdType.MESH
BF = jnp.bfloat16
F32 = jnp.float32

TOK, COT, XY, YX, OUT = 0, 2, 4, 6, 8
N_EX = 10


def nn(a, b):
    return jnp.dot(a, b, preferred_element_type=F32)


def nt(a, b):
    return lax.dot_general(a, b, (((1,), (1,)), ((), ())), preferred_element_type=F32)


def tn(a, b):
    return lax.dot_general(a, b, (((0,), (0,)), ((), ())), preferred_element_type=F32)


def norm_parts(v):
    c = v - jnp.mean(v, 0, keepdims=True)
    r = lax.rsqrt(jnp.mean(c * c, 0, keepdims=True) + 1e-05)
    return c * r, r


def norm_back(v, gain, e):
    xhat, r = norm_parts(v)
    dy = e * gain
    m1 = jnp.mean(dy, 0, keepdims=True)
    m2 = jnp.mean(dy * xhat, 0, keepdims=True)
    return r * (dy - m1 - xhat * m2)


def gelu_slope(x):
    k = 0.7978845608028654
    x2 = x * x
    t = jnp.tanh(k * x * (1.0 + 0.044715 * x2))
    return 0.5 * (1.0 + t) + (0.5 * k) * x * (1.0 - t * t) * (1.0 + 0.134145 * x2)


def kernel(
    tok, cot, gain_x, wqx, wox, gain_y, wqy, woy, gain_m, wup, wdn,
    out,
    wqx_v, wox_v, wqy_v, woy_v, wup_v, wdn_v,
    wqx_t, wox_t, wqy_t, woy_t, wup_t,
    gx_t, gy_t, gm_t,
    raw_t, raw_c, tokr, cotr, xl, cl, s1r, yl, g1r, g1x, gtx,
    xt, s1t, s2t, g2t, ct, ga, qkvx, qkvy, mixx, mixy, nrm, gmx, gqkv, gpre, ex, ey, ix, iy,
    rsem_raw, wsem, ssem, rsem,
):
    gx = lax.axis_index("gx")
    gy = lax.axis_index("gy")
    x_me = gx * 16 + gy
    y_me = gy * 16 + gx

    barrier = pltpu.get_barrier_semaphore()

    def loop(lo, hi, body):
        def step(i, carry):
            body(i)
            return carry

        lax.fori_loop(lo, hi, step, 0)

    gx_peers = [lax.rem(gx + p, 16) for p in range(16)]
    gy_peers = [lax.rem(gy + p, 16) for p in range(16)]

    for p in range(1, 16):
        for device in ((gx_peers[p], gy), (gx, gy_peers[p])):
            pl.semaphore_signal(barrier, inc=1, device_id=device, device_id_type=MESH)

    raws = [
        pltpu.make_async_copy(tok, raw_t, rsem_raw.at[0]),
        pltpu.make_async_copy(cot, raw_c, rsem_raw.at[1]),
    ]
    weights = (
        (wqx, wqx_v), (wox, wox_v), (wqy, wqy_v), (woy, woy_v), (wup, wup_v), (wdn, wdn_v)
    )
    loads = [pltpu.make_async_copy(s, d, wsem.at[i]) for i, (s, d) in enumerate(weights)]
    for load in raws + loads:
        load.start()

    def put(src, dst, device, k):
        pltpu.make_async_remote_copy(
            src_ref=src, dst_ref=dst, send_sem=ssem.at[k], recv_sem=rsem.at[k],
            device_id=device, device_id_type=MESH,
        ).start()

    def keep(src, dst, k):
        pltpu.make_async_copy(src, dst, rsem.at[k]).start()

    def arrived(k):
        pltpu.make_async_copy(yl.at[0], yl.at[0], rsem.at[k]).wait()

    def sent(k, tokens):
        part = yl.at[0, pl.ds(0, tokens)]
        pltpu.make_async_copy(part, part, ssem.at[k]).wait()

    def send_tok(c):
        dst = xl.at[c, gx]
        keep(tokr.at[c, gx], dst, TOK + c)
        for q in gx_peers[1:]:
            put(tokr.at[c, q], dst, (q, gy), TOK + c)

    def send_cot(c):
        dst = cl.at[c, gy]
        keep(cotr.at[c, gy], dst, COT + c)
        for q in gy_peers[1:]:
            put(cotr.at[c, q], dst, (gx, q), COT + c)

    def send_out(c):
        dst = out.at[gx, c]
        keep(gtx.at[c, gx], dst, OUT + c)
        for q in gx_peers[1:]:
            put(gtx.at[c, q], dst, (q, gy), OUT + c)

    def send_all(src, dst, row, me, k, c):
        keep(src.at[c, row(gx, gy)], dst.at[c, me], k + c)
        for q in gy_peers[1:]:
            put(src.at[c, row(gx, q)], dst.at[c, me], (gx, q), k + c)

        def body(i):
            a = lax.rem(gx + i, 16)
            for q in gy_peers:
                put(src.at[c, row(a, q)], dst.at[c, me], (a, q), k + c)

        loop(1, 16, body)

    def send_xy(c):
        send_all(s1r, yl, lambda a, b: a * 16 + b, y_me, XY, c)

    def send_yx(c):
        send_all(g1r, g1x, lambda a, b: b * 16 + a, x_me, YX, c)

    def split(raw, dst, swap):
        r = lax.broadcasted_iota(jnp.int32, (N, D), 0)
        s = lax.broadcasted_iota(jnp.int32, (N, D), 1)
        at = (r % 16) * 16 + r // 16 if swap else r
        whole = raw[...].reshape(D, D)
        for c in range(2):
            pick = jnp.where(s == at * 2 + c, 1.0, 0.0).astype(BF)
            dst[c] = nn(pick, whole).astype(BF).reshape(16, 16, D)

    def flip(src, dst, cols):
        def body(i):
            s = pl.multiple_of(i * 256, 256)
            dst[pl.ds(s, 256), :] = jnp.transpose(src[:, pl.ds(s, 256)])

        loop(0, cols // 256, body)

    raws[0].wait()
    split(raw_t, tokr, True)
    raws[1].wait()
    split(raw_c, cotr, False)
    for g, gt in ((gain_x, gx_t), (gain_y, gy_t), (gain_m, gm_t)):
        col = jnp.transpose(jnp.broadcast_to(g[...], (128, D)))
        gt[:, :128] = col
        gt[:, 128:] = col
    loads[0].wait()
    flip(wqx_v, wqx_t, 1536)
    loads[1].wait()
    flip(wox_v, wox_t, D)

    pl.semaphore_wait(barrier, 30)
    send_tok(0)
    send_tok(1)
    send_cot(0)
    send_cot(1)

    loads[2].wait()
    flip(wqy_v, wqy_t, 1536)
    loads[3].wait()
    flip(woy_v, woy_t, D)
    loads[4].wait()
    flip(wup_v, wup_t, FF)
    loads[5].wait()

    def forward(src_t, gain_t, wq_t, wo_t, qkv, es, invs, mix, dst_t):
        xhat, _ = norm_parts(src_t[...].astype(F32))
        nrm[...] = (xhat * gain_t[...]).astype(BF)
        qkv[...] = nn(wq_t[...], nrm[...]).astype(BF)
        for h in range(HEADS):
            o = h * HD
            q = qkv[o : o + HD, :] * 0.125
            k = qkv[o + D : o + D + HD, :]
            v = qkv[o + 2 * D : o + 2 * D + HD, :]
            s = tn(k, q)
            e = jnp.exp(s - jnp.max(s, 0, keepdims=True))
            inv = 1.0 / jnp.sum(e, 0, keepdims=True)
            e = e.astype(BF)
            es[h] = e
            invs[h] = inv
            mix[o : o + HD, :] = (nn(v, e) * inv).astype(BF)
        dst_t[...] = (src_t[...].astype(F32) + nn(wo_t[...], mix[...])).astype(BF)

    def heads_back(qkv, es, invs, mix, grad_t, wo):
        gmx[...] = nn(wo[...], grad_t[...]).astype(BF)
        for h in range(HEADS):
            o = h * HD
            q = qkv[o : o + HD, :]
            k = qkv[o + D : o + D + HD, :]
            v = qkv[o + 2 * D : o + 2 * D + HD, :]
            inv = invs[h]
            gi = gmx[o : o + HD, :].astype(F32) * inv
            delta = jnp.sum(gi * mix[o : o + HD, :].astype(F32), 0, keepdims=True)
            gi = gi.astype(BF)
            e = es[h]
            ds = (e.astype(F32) * (tn(v, gi) - delta)).astype(BF)
            gqkv[o : o + HD, :] = (nn(k, ds) * 0.125).astype(BF)
            gqkv[o + D : o + D + HD, :] = (nt(q, ds) * 0.125).astype(BF)
            gqkv[o + 2 * D : o + 2 * D + HD, :] = nt(gi, e).astype(BF)

    def finish_back(src_t, grad_t, gain_t, wq):
        e = nn(wq[...], gqkv[...])
        return grad_t[...].astype(F32) + norm_back(src_t[...].astype(F32), gain_t[...], e)

    def x_fwd(c):
        arrived(TOK + c)
        xt[c] = jnp.transpose(xl[c].reshape(N, D))
        forward(xt.at[c], gx_t, wqx_t, wox_t, qkvx.at[c], ex.at[c], ix.at[c], mixx.at[c], s2t)
        s1r[c] = jnp.transpose(s2t[...]).reshape(N, 4, 128)
        send_xy(c)

    def y_act(c):
        arrived(COT + c)
        ct[c] = jnp.transpose(cl[c].reshape(N, D))
        ga[c] = nn(wdn_v[...], ct[c]).astype(BF)

    def y_fwd(c):
        arrived(XY + c)
        s1t[...] = jnp.transpose(yl[c].reshape(N, D))
        forward(s1t, gy_t, wqy_t, woy_t, qkvy, ey, iy, mixy, s2t)

    def y_mlp(c):
        xhat, _ = norm_parts(s2t[...].astype(F32))
        nrm[...] = (xhat * gm_t[...]).astype(BF)
        gpre[...] = (
            ga[c].astype(F32) * gelu_slope(nn(wup_t[...], nrm[...]))
        ).astype(BF)
        e = nn(wup_v[...], gpre[...])
        g2t[...] = (
            ct[c].astype(F32) + norm_back(s2t[...].astype(F32), gm_t[...], e)
        ).astype(BF)

    def y_bwd(c):
        heads_back(qkvy, ey, iy, mixy, g2t, woy_v)
        g = finish_back(s1t, g2t, gy_t, wqy_v).astype(BF)
        g1r[c] = jnp.transpose(g).reshape(N, 4, 128)
        send_yx(c)

    def x_bwd(c):
        arrived(YX + c)
        g2t[...] = jnp.transpose(g1x[c].reshape(N, D))
        heads_back(qkvx.at[c], ex.at[c], ix.at[c], mixx.at[c], g2t, wox_v)
        g = finish_back(xt.at[c], g2t, gx_t, wqx_v).astype(BF)
        gtx[c] = jnp.transpose(g).reshape(16, 16, D)
        send_out(c)

    x_fwd(0)
    x_fwd(1)
    y_act(0)
    y_act(1)
    y_fwd(0)
    y_mlp(0)
    y_bwd(0)
    y_fwd(1)
    y_mlp(1)
    y_bwd(1)
    x_bwd(0)
    x_bwd(1)

    for c in range(2):
        arrived(OUT + c)
        sent(TOK + c, 240)
        sent(COT + c, 240)
        sent(XY + c, 255)
        sent(YX + c, 255)
        sent(OUT + c, 240)


def local(
    tokens, cotangent, gain_x, w_qkv_x, w_out_x, gain_y, w_qkv_y, w_out_y, gain_mlp, w_up, w_down
):
    any_spec = pl.BlockSpec(memory_space=pl.ANY)
    vm = pl.BlockSpec(memory_space=pltpu.VMEM)
    V = pltpu.VMEM
    scratch = [
        V((D, 1536), BF), V((D, D), BF), V((D, 1536), BF), V((D, D), BF), V((D, FF), BF),
        V((FF, D), BF),
        V((1536, D), BF), V((D, D), BF), V((1536, D), BF), V((D, D), BF), V((FF, D), BF),
        V((D, N), F32), V((D, N), F32), V((D, N), F32),
        V((16, 16, 2, D), BF), V((16, 16, 2, D), BF),
        V((2, 16, 16, D), BF), V((2, 16, 16, D), BF),
        V((2, 16, 16, D), BF), V((2, 16, 16, D), BF),
        V((2, N, 4, 128), BF), V((2, N, 4, 128), BF),
        V((2, N, 4, 128), BF), V((2, N, 4, 128), BF),
        V((2, 16, 16, D), BF),
        V((2, D, N), BF),
        V((D, N), BF), V((D, N), BF), V((D, N), BF),
        V((2, D, N), BF), V((2, FF, N), BF),
        V((2, 1536, N), BF), V((1536, N), BF),
        V((2, D, N), BF), V((D, N), BF), V((D, N), BF), V((D, N), BF),
        V((1536, N), BF), V((FF, N), BF),
        V((2, HEADS, N, N), BF), V((HEADS, N, N), BF),
        V((2, HEADS, 1, N), F32), V((HEADS, 1, N), F32),
        pltpu.SemaphoreType.DMA((2,)),
        pltpu.SemaphoreType.DMA((6,)),
        pltpu.SemaphoreType.DMA((N_EX,)),
        pltpu.SemaphoreType.DMA((N_EX,)),
    ]
    res = pl.pallas_call(
        kernel,
        out_shape=jax.ShapeDtypeStruct((16, 2, 16, D), BF),
        in_specs=[any_spec, any_spec, vm, any_spec, any_spec, vm, any_spec, any_spec, vm,
                  any_spec, any_spec],
        out_specs=any_spec,
        scratch_shapes=scratch,
        compiler_params=pltpu.CompilerParams(
            collective_id=0, has_side_effects=True, vmem_limit_bytes=60 * 1024 * 1024
        ),
        name="axial_grad",
    )(
        tokens, cotangent, gain_x.reshape(1, D), w_qkv_x, w_out_x, gain_y.reshape(1, D), w_qkv_y,
        w_out_y, gain_mlp.reshape(1, D), w_up, w_down,
    )
    return jnp.transpose(res, (2, 0, 1, 3))


def solution(mesh):
    in_specs = (P("gx", "gy", None, None), P("gx", "gy", None, None)) + (P(),) * 9
    out_specs = P("gx", "gy", None, None)
    return jax.shard_map(local, mesh=mesh, in_specs=in_specs, out_specs=out_specs, check_vma=False)
```

```python
import jax
import jax.numpy as jnp
from jax import lax
from jax.experimental import pallas as pl
from jax.experimental.pallas import tpu as pltpu
from jax.sharding import PartitionSpec as P

D = 512
HEADS = 8
HD = 64
FF = 2048
N = 256
MESH = pl.DeviceIdType.MESH
BF = jnp.bfloat16
F32 = jnp.float32

TOK, COT, XY, YX, OUT = 0, 2, 4, 6, 8
N_EX = 10


def nn(a, b):
    return jnp.dot(a, b, preferred_element_type=F32)


def nt(a, b):
    return lax.dot_general(a, b, (((1,), (1,)), ((), ())), preferred_element_type=F32)


def tn(a, b):
    return lax.dot_general(a, b, (((0,), (0,)), ((), ())), preferred_element_type=F32)


def norm_parts(v):
    c = v - jnp.mean(v, 0, keepdims=True)
    r = lax.rsqrt(jnp.mean(c * c, 0, keepdims=True) + 1e-05)
    return c * r, r


def norm_back(v, gain, e):
    xhat, r = norm_parts(v)
    dy = e * gain
    m1 = jnp.mean(dy, 0, keepdims=True)
    m2 = jnp.mean(dy * xhat, 0, keepdims=True)
    return r * (dy - m1 - xhat * m2)


def gelu_slope(x):
    k = 0.7978845608028654
    x2 = x * x
    t = jnp.tanh(k * x * (1.0 + 0.044715 * x2))
    return 0.5 * (1.0 + t) + (0.5 * k) * x * (1.0 - t * t) * (1.0 + 0.134145 * x2)


def kernel(
    tok, cot, gain_x, wqx, wox, gain_y, wqy, woy, gain_m, wup, wdn,
    out,
    wqx_v, wox_v, wqy_v, woy_v, wup_v, wdn_v,
    wqx_t, wox_t, wqy_t, woy_t, wup_t,
    gx_t, gy_t, gm_t, gain_v,
    raw_t, raw_c, tokr, cotr, xl, cl, s1r, yl, g1r, g1x, gtx,
    xt, s1t, s2t, g2t, ct, ga, qkvx, qkvy, mixx, mixy, nrm, gmx, gqkv, gpre, ex, ey, ix, iy,
    rsem_raw, wsem, ssem, rsem,
):
    gx = lax.axis_index("gx")
    gy = lax.axis_index("gy")
    gyo = lax.rem(gy + 8, 16)
    x_me = gx * 16 + gy
    y_me = gyo * 16 + gx
    X, zh = gx // 4, lax.rem(gx, 4)
    zl, Yc = gy // 8, lax.rem(gy, 8)
    z = zh * 2 + zl

    barrier = pltpu.get_barrier_semaphore()

    def loop(lo, hi, body):
        def step(i, carry):
            body(i)
            return carry

        lax.fori_loop(lo, hi, step, 0)

    row_peers = [
        lax.rem(X + dx, 4) * 4 + lax.rem(zh + zl + dz, 4) for dz in (1, 2, 3, 0) for dx in (2, 1, 3, 0)
    ]
    near = [
        lax.rem(Yc // 2 + dy, 4) * 2 + lax.rem(Yc + dc, 2) for dy in (2, 1, 3, 0) for dc in (1, 0)
    ]
    gy_peers = [lax.rem(zl + dl, 2) * 8 + q for dl in (1, 0) for q in near]

    for q in row_peers:
        pl.semaphore_signal(barrier, inc=1, device_id=(q, gyo), device_id_type=MESH)
    for q in gy_peers[:-1]:
        pl.semaphore_signal(barrier, inc=1, device_id=(gx, q), device_id_type=MESH)

    raws = [
        pltpu.make_async_copy(tok, raw_t, rsem_raw.at[0]),
        pltpu.make_async_copy(cot, raw_c, rsem_raw.at[1]),
        pltpu.make_async_copy(gain_x, gain_v.at[0], rsem_raw.at[2]),
        pltpu.make_async_copy(gain_y, gain_v.at[1], rsem_raw.at[3]),
        pltpu.make_async_copy(gain_m, gain_v.at[2], rsem_raw.at[4]),
    ]
    weights = (
        (wqx, wqx_v), (wox, wox_v), (wqy, wqy_v), (woy, woy_v), (wup, wup_v), (wdn, wdn_v)
    )
    loads = [pltpu.make_async_copy(s, d, wsem.at[i]) for i, (s, d) in enumerate(weights)]
    for load in raws + loads:
        load.start()

    def put(src, dst, device, k):
        pltpu.make_async_remote_copy(
            src_ref=src, dst_ref=dst, send_sem=ssem.at[k], recv_sem=rsem.at[k],
            device_id=device, device_id_type=MESH,
        ).start()

    def keep(src, dst, k):
        pltpu.make_async_copy(src, dst, rsem.at[k]).start()

    def arrived(k):
        pltpu.make_async_copy(yl.at[0], yl.at[0], rsem.at[k]).wait()

    def sent(k, tokens):
        part = yl.at[0, pl.ds(0, tokens)]
        pltpu.make_async_copy(part, part, ssem.at[k]).wait()

    def send_tok(c):
        for q in row_peers:
            put(tokr.at[c, q], xl.at[c, gx], (q, gyo), TOK + c)

    def send_cot(c):
        dst = cl.at[c, gy]
        keep(cotr.at[c, gy], dst, COT + c)
        for q in gy_peers[:-1]:
            put(cotr.at[c, q], dst, (gx, q), COT + c)

    def send_out(c):
        for q in row_peers:
            put(gtx.at[c, q], out.at[gx, c], (q, gyo), OUT + c)

    def outward(k, half):
        return half + jnp.where(k % 2 == 0, k // 2, -((k + 1) // 2))

    def send_all(src, dst, row, me, k, c):
        keep(src.at[c, row(gx, gy)], dst.at[c, me], k + c)

        def body(i, last=0):
            zz = lax.rem(z + outward(i // 4, 4), 8)
            a = lax.rem(X + outward(i % 4, 2), 4) * 4 + zz // 2
            b = (zz % 2) * 8
            for q in near[: 8 - last]:
                put(src.at[c, row(a, b + q)], dst.at[c, me], (a, b + q), k + c)

        loop(0, 31, body)
        body(31, 1)

    def send_xy(c):
        send_all(s1r, yl, lambda a, b: a * 16 + b, y_me, XY, c)

    def send_yx(c):
        send_all(g1r, g1x, lambda a, b: lax.rem(b + 8, 16) * 16 + a, x_me, YX, c)

    def split(raw, dst, swap):
        r = lax.broadcasted_iota(jnp.int32, (N, D), 0)
        s = lax.broadcasted_iota(jnp.int32, (N, D), 1)
        at = (r % 16) * 16 + r // 16 if swap else r
        whole = raw[...].reshape(D, D)
        for c in range(2):
            pick = jnp.where(s == at * 2 + c, 1.0, 0.0).astype(BF)
            dst[c] = nn(pick, whole).astype(BF).reshape(16, 16, D)

    def flip(src, dst, cols):
        def body(i):
            s = pl.multiple_of(i * 256, 256)
            dst[pl.ds(s, 256), :] = jnp.transpose(src[:, pl.ds(s, 256)])

        loop(0, cols // 256, body)

    raws[0].wait()
    split(raw_t, tokr, True)
    raws[1].wait()
    split(raw_c, cotr, False)
    for i, gt in enumerate((gx_t, gy_t, gm_t)):
        raws[2 + i].wait()
        col = jnp.transpose(jnp.broadcast_to(gain_v[i], (128, D)))
        gt[:, :128] = col
        gt[:, 128:] = col
    loads[0].wait()
    flip(wqx_v, wqx_t, 1536)
    loads[1].wait()
    flip(wox_v, wox_t, D)

    pl.semaphore_wait(barrier, 31)
    send_tok(0)
    send_cot(0)
    send_tok(1)

    loads[2].wait()
    flip(wqy_v, wqy_t, 1536)
    loads[3].wait()
    flip(woy_v, woy_t, D)
    loads[4].wait()
    flip(wup_v, wup_t, FF)
    loads[5].wait()

    def forward(src_t, gain_t, wq_t, wo_t, qkv, es, invs, mix, dst_t):
        xhat, _ = norm_parts(src_t[...].astype(F32))
        nrm[...] = (xhat * gain_t[...]).astype(BF)
        qkv[...] = nn(wq_t[...], nrm[...]).astype(BF)
        for h in range(HEADS):
            o = h * HD
            q = qkv[o : o + HD, :] * 0.125
            k = qkv[o + D : o + D + HD, :]
            v = qkv[o + 2 * D : o + 2 * D + HD, :]
            s = tn(k, q)
            e = jnp.exp(s - jnp.max(s, 0, keepdims=True))
            inv = 1.0 / jnp.sum(e, 0, keepdims=True)
            e = e.astype(BF)
            es[h] = e
            invs[h] = inv
            mix[o : o + HD, :] = (nn(v, e) * inv).astype(BF)
        dst_t[...] = (src_t[...].astype(F32) + nn(wo_t[...], mix[...])).astype(BF)

    def heads_back(qkv, es, invs, mix, grad_t, wo):
        gmx[...] = nn(wo[...], grad_t[...]).astype(BF)
        for h in range(HEADS):
            o = h * HD
            q = qkv[o : o + HD, :]
            k = qkv[o + D : o + D + HD, :]
            v = qkv[o + 2 * D : o + 2 * D + HD, :]
            inv = invs[h]
            gi = gmx[o : o + HD, :].astype(F32) * inv
            delta = jnp.sum(gi * mix[o : o + HD, :].astype(F32), 0, keepdims=True)
            gi = gi.astype(BF)
            e = es[h]
            ds = (e.astype(F32) * (tn(v, gi) - delta)).astype(BF)
            gqkv[o : o + HD, :] = (nn(k, ds) * 0.125).astype(BF)
            gqkv[o + D : o + D + HD, :] = (nt(q, ds) * 0.125).astype(BF)
            gqkv[o + 2 * D : o + 2 * D + HD, :] = nt(gi, e).astype(BF)

    def finish_back(src_t, grad_t, gain_t, wq):
        e = nn(wq[...], gqkv[...])
        return grad_t[...].astype(F32) + norm_back(src_t[...].astype(F32), gain_t[...], e)

    def x_fwd(c):
        arrived(TOK + c)
        xt[c] = jnp.transpose(xl[c].reshape(N, D))
        forward(xt.at[c], gx_t, wqx_t, wox_t, qkvx.at[c], ex.at[c], ix.at[c], mixx.at[c], s2t)
        s1r[c] = jnp.transpose(s2t[...]).reshape(N, 4, 128)
        send_xy(c)

    def y_act(c):
        arrived(COT + c)
        ct[c] = jnp.transpose(cl[c].reshape(N, D))
        ga[c] = nn(wdn_v[...], ct[c]).astype(BF)

    def y_fwd(c):
        arrived(XY + c)
        s1t[...] = jnp.transpose(yl[c].reshape(N, D))
        forward(s1t, gy_t, wqy_t, woy_t, qkvy, ey, iy, mixy, s2t)

    def y_mlp(c):
        xhat, _ = norm_parts(s2t[...].astype(F32))
        nrm[...] = (xhat * gm_t[...]).astype(BF)
        gpre[...] = (
            ga[c].astype(F32) * gelu_slope(nn(wup_t[...], nrm[...]))
        ).astype(BF)
        e = nn(wup_v[...], gpre[...])
        g2t[...] = (
            ct[c].astype(F32) + norm_back(s2t[...].astype(F32), gm_t[...], e)
        ).astype(BF)

    def y_bwd(c):
        heads_back(qkvy, ey, iy, mixy, g2t, woy_v)
        g = finish_back(s1t, g2t, gy_t, wqy_v).astype(BF)
        g1r[c] = jnp.transpose(g).reshape(N, 4, 128)
        send_yx(c)

    def x_bwd(c):
        arrived(YX + c)
        g2t[...] = jnp.transpose(g1x[c].reshape(N, D))
        heads_back(qkvx.at[c], ex.at[c], ix.at[c], mixx.at[c], g2t, wox_v)
        g = finish_back(xt.at[c], g2t, gx_t, wqx_v).astype(BF)
        gtx[c] = jnp.transpose(g).reshape(16, 16, D)
        send_out(c)

    x_fwd(0)
    send_cot(1)
    x_fwd(1)
    y_act(0)
    y_act(1)
    y_fwd(0)
    y_mlp(0)
    y_bwd(0)
    y_fwd(1)
    y_mlp(1)
    y_bwd(1)
    x_bwd(0)
    x_bwd(1)

    for c in range(2):
        arrived(OUT + c)
        sent(TOK + c, 256)
        sent(COT + c, 240)
        sent(XY + c, 255)
        sent(YX + c, 255)
        sent(OUT + c, 256)


def local(
    tokens, cotangent, gain_x, w_qkv_x, w_out_x, gain_y, w_qkv_y, w_out_y, gain_mlp, w_up, w_down
):
    any_spec = pl.BlockSpec(memory_space=pl.ANY)
    V = pltpu.VMEM
    scratch = [
        V((D, 1536), BF), V((D, D), BF), V((D, 1536), BF), V((D, D), BF), V((D, FF), BF),
        V((FF, D), BF),
        V((1536, D), BF), V((D, D), BF), V((1536, D), BF), V((D, D), BF), V((FF, D), BF),
        V((D, N), F32), V((D, N), F32), V((D, N), F32), V((3, 1, D), F32),
        V((16, 16, 2, D), BF), V((16, 16, 2, D), BF),
        V((2, 16, 16, D), BF), V((2, 16, 16, D), BF),
        V((2, 16, 16, D), BF), V((2, 16, 16, D), BF),
        V((2, N, 4, 128), BF), V((2, N, 4, 128), BF),
        V((2, N, 4, 128), BF), V((2, N, 4, 128), BF),
        V((2, 16, 16, D), BF),
        V((2, D, N), BF),
        V((D, N), BF), V((D, N), BF), V((D, N), BF),
        V((2, D, N), BF), V((2, FF, N), BF),
        V((2, 1536, N), BF), V((1536, N), BF),
        V((2, D, N), BF), V((D, N), BF), V((D, N), BF), V((D, N), BF),
        V((1536, N), BF), V((FF, N), BF),
        V((2, HEADS, N, N), BF), V((HEADS, N, N), BF),
        V((2, HEADS, 1, N), F32), V((HEADS, 1, N), F32),
        pltpu.SemaphoreType.DMA((5,)),
        pltpu.SemaphoreType.DMA((6,)),
        pltpu.SemaphoreType.DMA((N_EX,)),
        pltpu.SemaphoreType.DMA((N_EX,)),
    ]
    res = pl.pallas_call(
        kernel,
        out_shape=jax.ShapeDtypeStruct((16, 2, 16, D), BF),
        in_specs=[any_spec] * 11,
        out_specs=any_spec,
        scratch_shapes=scratch,
        compiler_params=pltpu.CompilerParams(
            collective_id=0, has_side_effects=True, vmem_limit_bytes=60 * 1024 * 1024
        ),
        name="axial_grad",
    )(
        tokens, cotangent, gain_x.reshape(1, D), w_qkv_x, w_out_x, gain_y.reshape(1, D), w_qkv_y,
        w_out_y, gain_mlp.reshape(1, D), w_up, w_down,
    )
    return jnp.transpose(res, (2, 0, 1, 3))


def solution(mesh):
    in_specs = (P("gx", "gy", None, None), P("gx", "gy", None, None)) + (P(),) * 9
    out_specs = P("gx", "gy", None, None)
    return jax.shard_map(local, mesh=mesh, in_specs=in_specs, out_specs=out_specs, check_vma=False)
```

```python
import jax
import jax.numpy as jnp
from jax import lax
from jax.experimental import pallas as pl
from jax.experimental.pallas import tpu as pltpu
from jax.sharding import PartitionSpec as P

D = 512
HEADS = 8
HD = 64
FF = 2048
N = 256
MESH = pl.DeviceIdType.MESH
BF = jnp.bfloat16
F32 = jnp.float32

TOK, COT, XY, YX, OUT = 0, 2, 4, 6, 8
N_EX = 10


def nn(a, b):
    return jnp.dot(a, b, preferred_element_type=F32)


def nt(a, b):
    return lax.dot_general(a, b, (((1,), (1,)), ((), ())), preferred_element_type=F32)


def tn(a, b):
    return lax.dot_general(a, b, (((0,), (0,)), ((), ())), preferred_element_type=F32)


def norm_parts(v):
    c = v - jnp.mean(v, 0, keepdims=True)
    r = lax.rsqrt(jnp.mean(c * c, 0, keepdims=True) + 1e-05)
    return c * r, r


def norm_back(v, gain, e):
    xhat, r = norm_parts(v)
    dy = e * gain
    m1 = jnp.mean(dy, 0, keepdims=True)
    m2 = jnp.mean(dy * xhat, 0, keepdims=True)
    return r * (dy - m1 - xhat * m2)


def gelu_slope(x):
    k = 0.7978845608028654
    p = (6 * 0.044715 * k) * (x * x)
    a = 0.5 + 0.5 * jnp.tanh(x * (p * (1.0 / 6.0) + k))
    return a + a * (1.0 - a) * (x * (p + 2.0 * k))


def kernel(
    tok, cot, gain_x, wqx, wox, gain_y, wqy, woy, gain_m, wup, wdn,
    out,
    wqx_v, wox_v, wqy_v, woy_v, wup_v, wdn_v,
    wqx_t, wox_t, wqy_t, woy_t, wup_t,
    gx_t, gy_t, gm_t, gain_v,
    raw_t, raw_c, tokr, cotr, xl, cl, s1r, yl, g1r, g1x, gtx,
    xt, s1t, s2t, g2t, ct, ga, qkvx, qkvy, mixx, mixy, nrm, gmx, gqkv, gpre, ex, ey, ix, iy, sc, dsb, dlt,
    rsem_raw, wsem, ssem, rsem,
):
    gx = lax.axis_index("gx")
    gy = lax.axis_index("gy")
    gyo = lax.rem(gy + 8, 16)
    x_me = gx * 16 + gy
    y_me = gyo * 16 + gx
    X, zh = gx // 4, lax.rem(gx, 4)
    zl, Yc = gy // 8, lax.rem(gy, 8)
    z = zh * 2 + zl

    barrier = pltpu.get_barrier_semaphore()

    def loop(lo, hi, body):
        def step(i, carry):
            body(i)
            return carry

        lax.fori_loop(lo, hi, step, 0)

    row_peers = [
        lax.rem(X + dx, 4) * 4 + lax.rem(zh + zl + dz, 4) for dz in (1, 2, 3, 0) for dx in (2, 1, 3, 0)
    ]
    near = [
        lax.rem(Yc // 2 + dy, 4) * 2 + lax.rem(Yc + dc, 2) for dy in (2, 1, 3, 0) for dc in (1, 0)
    ]
    gy_peers = [lax.rem(zl + dl, 2) * 8 + q for dl in (1, 0) for q in near]

    for q in row_peers:
        pl.semaphore_signal(barrier, inc=1, device_id=(q, gyo), device_id_type=MESH)
    for q in gy_peers[:-1]:
        pl.semaphore_signal(barrier, inc=1, device_id=(gx, q), device_id_type=MESH)

    raws = [
        pltpu.make_async_copy(tok, raw_t, rsem_raw.at[0]),
        pltpu.make_async_copy(cot, raw_c, rsem_raw.at[1]),
        pltpu.make_async_copy(gain_x, gain_v.at[0], rsem_raw.at[2]),
        pltpu.make_async_copy(gain_y, gain_v.at[1], rsem_raw.at[3]),
        pltpu.make_async_copy(gain_m, gain_v.at[2], rsem_raw.at[4]),
    ]
    weights = (
        (wqx, wqx_v), (wox, wox_v), (wqy, wqy_v), (woy, woy_v), (wup, wup_v), (wdn, wdn_v)
    )
    loads = [pltpu.make_async_copy(s, d, wsem.at[i]) for i, (s, d) in enumerate(weights)]
    for load in raws + loads:
        load.start()

    def put(src, dst, device, k):
        pltpu.make_async_remote_copy(
            src_ref=src, dst_ref=dst, send_sem=ssem.at[k], recv_sem=rsem.at[k],
            device_id=device, device_id_type=MESH,
        ).start()

    def keep(src, dst, k):
        pltpu.make_async_copy(src, dst, rsem.at[k]).start()

    def arrived(k):
        pltpu.make_async_copy(yl.at[0], yl.at[0], rsem.at[k]).wait()

    def sent(k, tokens):
        part = yl.at[0, pl.ds(0, tokens)]
        pltpu.make_async_copy(part, part, ssem.at[k]).wait()

    def send_tok(c):
        for q in row_peers:
            put(tokr.at[c, q], xl.at[c, gx], (q, gyo), TOK + c)

    def send_cot(c):
        dst = cl.at[c, gy]
        keep(cotr.at[c, gy], dst, COT + c)
        for q in gy_peers[:-1]:
            put(cotr.at[c, q], dst, (gx, q), COT + c)

    def send_out(c):
        for q in row_peers:
            put(gtx.at[c, q], out.at[gx, c], (q, gyo), OUT + c)

    def outward(k, half):
        return half + jnp.where(k % 2 == 0, k // 2, -((k + 1) // 2))

    def send_all(src, dst, row, me, k, c):
        keep(src.at[c, row(gx, gy)], dst.at[c, me], k + c)

        def body(i, last=0):
            zz = lax.rem(z + outward(i // 4, 4), 8)
            a = lax.rem(X + outward(i % 4, 2), 4) * 4 + zz // 2
            b = (zz % 2) * 8
            for q in near[: 8 - last]:
                put(src.at[c, row(a, b + q)], dst.at[c, me], (a, b + q), k + c)

        loop(0, 31, body)
        body(31, 1)

    def send_xy(c):
        send_all(s1r, yl, lambda a, b: a * 16 + b, y_me, XY, c)

    def send_yx(c):
        send_all(g1r, g1x, lambda a, b: lax.rem(b + 8, 16) * 16 + a, x_me, YX, c)

    def split(raw, dst, swap):
        r = lax.broadcasted_iota(jnp.int32, (N, D), 0)
        s = lax.broadcasted_iota(jnp.int32, (N, D), 1)
        at = (r % 16) * 16 + r // 16 if swap else r
        whole = raw[...].reshape(D, D)
        for c in range(2):
            pick = jnp.where(s == at * 2 + c, 1.0, 0.0).astype(BF)
            dst[c] = nn(pick, whole).astype(BF).reshape(16, 16, D)

    def flip(src, dst, cols):
        def body(i):
            s = pl.multiple_of(i * 256, 256)
            dst[pl.ds(s, 256), :] = jnp.transpose(src[:, pl.ds(s, 256)])

        loop(0, cols // 256, body)

    raws[0].wait()
    split(raw_t, tokr, True)
    raws[1].wait()
    split(raw_c, cotr, False)
    for i, gt in enumerate((gx_t, gy_t, gm_t)):
        raws[2 + i].wait()
        col = jnp.transpose(jnp.broadcast_to(gain_v[i], (128, D)))
        gt[:, :128] = col
        gt[:, 128:] = col
    loads[0].wait()
    flip(wqx_v, wqx_t, 1536)
    loads[1].wait()
    flip(wox_v, wox_t, D)

    pl.semaphore_wait(barrier, 31)
    send_tok(0)
    send_cot(0)
    send_tok(1)

    loads[2].wait()
    flip(wqy_v, wqy_t, 1536)
    loads[3].wait()
    flip(woy_v, woy_t, D)
    loads[4].wait()
    flip(wup_v, wup_t, FF)
    loads[5].wait()

    def forward(src_t, gain_t, wq_t, wo_t, qkv, es, invs, mix, dst_t):
        xhat, _ = norm_parts(src_t[...].astype(F32))
        nrm[...] = (xhat * gain_t[...]).astype(BF)
        qkv[...] = nn(wq_t[...], nrm[...]).astype(BF)
        for h in range(HEADS):
            o = h * HD
            sc[h] = tn(qkv[o + D : o + D + HD, :], qkv[o : o + HD, :] * 0.125)
        for h in range(HEADS):
            for t in (0, 128):
                s = sc[h, :, t : t + 128]
                e = jnp.exp(s - jnp.max(s, 0, keepdims=True))
                invs[h, :, t : t + 128] = 1.0 / jnp.sum(e, 0, keepdims=True)
                es[h, :, t : t + 128] = e.astype(BF)
        for h in range(HEADS):
            o = h * HD
            v = qkv[o + 2 * D : o + 2 * D + HD, :]
            mix[o : o + HD, :] = (nn(v, es[h]) * invs[h]).astype(BF)
        dst_t[...] = (src_t[...].astype(F32) + nn(wo_t[...], mix[...])).astype(BF)

    def heads_back(qkv, es, invs, mix, grad_t, wo):
        gmx[...] = nn(wo[...], grad_t[...]).astype(BF)
        for h in range(HEADS):
            o = h * HD
            gi = gmx[o : o + HD, :].astype(F32) * invs[h]
            dlt[h] = jnp.sum(gi * mix[o : o + HD, :].astype(F32), 0, keepdims=True)
            gi = gi.astype(BF)
            gmx[o : o + HD, :] = gi
            sc[h] = tn(qkv[o + 2 * D : o + 2 * D + HD, :], gi)
        for h in range(HEADS):
            o = h * HD
            gqkv[o + 2 * D : o + 2 * D + HD, :] = nt(gmx[o : o + HD, :], es[h]).astype(BF)
        for h in range(HEADS):
            dsb[h] = (es[h].astype(F32) * (sc[h] - dlt[h])).astype(BF)
        for h in range(HEADS):
            o = h * HD
            gqkv[o : o + HD, :] = (nn(qkv[o + D : o + D + HD, :], dsb[h]) * 0.125).astype(BF)
            gqkv[o + D : o + D + HD, :] = (nt(qkv[o : o + HD, :], dsb[h]) * 0.125).astype(BF)

    def finish_back(src_t, grad_t, gain_t, wq):
        e = nn(wq[...], gqkv[...])
        return grad_t[...].astype(F32) + norm_back(src_t[...].astype(F32), gain_t[...], e)

    def x_fwd(c):
        arrived(TOK + c)
        xt[c] = jnp.transpose(xl[c].reshape(N, D))
        forward(xt.at[c], gx_t, wqx_t, wox_t, qkvx.at[c], ex.at[c], ix.at[c], mixx.at[c], s2t)
        s1r[c] = jnp.transpose(s2t[...]).reshape(N, 4, 128)
        send_xy(c)

    def y_act(c):
        arrived(COT + c)
        ct[c] = jnp.transpose(cl[c].reshape(N, D))
        ga[c] = nn(wdn_v[...], ct[c]).astype(BF)

    def y_fwd(c):
        arrived(XY + c)
        s1t[...] = jnp.transpose(yl[c].reshape(N, D))
        forward(s1t, gy_t, wqy_t, woy_t, qkvy, ey, iy, mixy, s2t)

    def y_mlp(c):
        xhat, _ = norm_parts(s2t[...].astype(F32))
        nrm[...] = (xhat * gm_t[...]).astype(BF)
        gpre[...] = (
            ga[c].astype(F32) * gelu_slope(nn(wup_t[...], nrm[...]))
        ).astype(BF)
        e = nn(wup_v[...], gpre[...])
        g2t[...] = (
            ct[c].astype(F32) + norm_back(s2t[...].astype(F32), gm_t[...], e)
        ).astype(BF)

    def y_bwd(c):
        heads_back(qkvy, ey, iy, mixy, g2t, woy_v)
        g = finish_back(s1t, g2t, gy_t, wqy_v).astype(BF)
        g1r[c] = jnp.transpose(g).reshape(N, 4, 128)
        send_yx(c)

    def x_bwd(c):
        arrived(YX + c)
        g2t[...] = jnp.transpose(g1x[c].reshape(N, D))
        heads_back(qkvx.at[c], ex.at[c], ix.at[c], mixx.at[c], g2t, wox_v)
        g = finish_back(xt.at[c], g2t, gx_t, wqx_v).astype(BF)
        gtx[c] = jnp.transpose(g).reshape(16, 16, D)
        send_out(c)

    x_fwd(0)
    send_cot(1)
    x_fwd(1)
    y_act(0)
    y_act(1)
    y_fwd(0)
    y_mlp(0)
    y_bwd(0)
    y_fwd(1)
    y_mlp(1)
    y_bwd(1)
    x_bwd(0)
    x_bwd(1)

    for c in range(2):
        arrived(OUT + c)
        sent(TOK + c, 256)
        sent(COT + c, 240)
        sent(XY + c, 255)
        sent(YX + c, 255)
        sent(OUT + c, 256)


def local(
    tokens, cotangent, gain_x, w_qkv_x, w_out_x, gain_y, w_qkv_y, w_out_y, gain_mlp, w_up, w_down
):
    any_spec = pl.BlockSpec(memory_space=pl.ANY)
    V = pltpu.VMEM
    scratch = [
        V((D, 1536), BF), V((D, D), BF), V((D, 1536), BF), V((D, D), BF), V((D, FF), BF),
        V((FF, D), BF),
        V((1536, D), BF), V((D, D), BF), V((1536, D), BF), V((D, D), BF), V((FF, D), BF),
        V((D, N), F32), V((D, N), F32), V((D, N), F32), V((3, 1, D), F32),
        V((16, 16, 2, D), BF), V((16, 16, 2, D), BF),
        V((2, 16, 16, D), BF), V((2, 16, 16, D), BF),
        V((2, 16, 16, D), BF), V((2, 16, 16, D), BF),
        V((2, N, 4, 128), BF), V((2, N, 4, 128), BF),
        V((2, N, 4, 128), BF), V((2, N, 4, 128), BF),
        V((2, 16, 16, D), BF),
        V((2, D, N), BF),
        V((D, N), BF), V((D, N), BF), V((D, N), BF),
        V((2, D, N), BF), V((2, FF, N), BF),
        V((2, 1536, N), BF), V((1536, N), BF),
        V((2, D, N), BF), V((D, N), BF), V((D, N), BF), V((D, N), BF),
        V((1536, N), BF), V((FF, N), BF),
        V((2, HEADS, N, N), BF), V((HEADS, N, N), BF),
        V((2, HEADS, 1, N), F32), V((HEADS, 1, N), F32),
        V((HEADS, N, N), F32), V((HEADS, N, N), BF), V((HEADS, 1, N), F32),
        pltpu.SemaphoreType.DMA((5,)),
        pltpu.SemaphoreType.DMA((6,)),
        pltpu.SemaphoreType.DMA((N_EX,)),
        pltpu.SemaphoreType.DMA((N_EX,)),
    ]
    res = pl.pallas_call(
        kernel,
        out_shape=jax.ShapeDtypeStruct((16, 2, 16, D), BF),
        in_specs=[any_spec] * 11,
        out_specs=any_spec,
        scratch_shapes=scratch,
        compiler_params=pltpu.CompilerParams(
            collective_id=0, has_side_effects=True, vmem_limit_bytes=60 * 1024 * 1024
        ),
        name="axial_grad",
    )(
        tokens, cotangent, gain_x.reshape(1, D), w_qkv_x, w_out_x, gain_y.reshape(1, D), w_qkv_y,
        w_out_y, gain_mlp.reshape(1, D), w_up, w_down,
    )
    return jnp.transpose(res, (2, 0, 1, 3))


def solution(mesh):
    in_specs = (P("gx", "gy", None, None), P("gx", "gy", None, None)) + (P(),) * 9
    out_specs = P("gx", "gy", None, None)
    return jax.shard_map(local, mesh=mesh, in_specs=in_specs, out_specs=out_specs, check_vma=False)
```

```python
import jax
import jax.numpy as jnp
from jax import lax
from jax.experimental import pallas as pl
from jax.experimental.pallas import tpu as pltpu
from jax.sharding import PartitionSpec as P

D = 512
HEADS = 8
HD = 64
FF = 2048
N = 256
MESH = pl.DeviceIdType.MESH
BF = jnp.bfloat16
F32 = jnp.float32

TOK, COT, XY, YX, OUT = 0, 2, 4, 6, 8
N_EX = 10


def nn(a, b):
    return jnp.dot(a, b, preferred_element_type=F32)


def nt(a, b):
    return lax.dot_general(a, b, (((1,), (1,)), ((), ())), preferred_element_type=F32)


def tn(a, b):
    return lax.dot_general(a, b, (((0,), (0,)), ((), ())), preferred_element_type=F32)


def norm_parts(v):
    c = v - jnp.mean(v, 0, keepdims=True)
    r = lax.rsqrt(jnp.mean(c * c, 0, keepdims=True) + 1e-05)
    return c * r, r


def norm_back(v, gain, e):
    xhat, r = norm_parts(v)
    dy = e * gain
    m1 = jnp.mean(dy, 0, keepdims=True)
    m2 = jnp.mean(dy * xhat, 0, keepdims=True)
    return r * (dy - m1 - xhat * m2)


def gelu_slope(x):
    k = 0.7978845608028654
    p = (6 * 0.044715 * k) * (x * x)
    a = 0.5 + 0.5 * jnp.tanh(x * (p * (1.0 / 6.0) + k))
    return a + a * (1.0 - a) * (x * (p + 2.0 * k))


def kernel(
    tok, cot, gain_x, wqx, wox, gain_y, wqy, woy, gain_m, wup, wdn,
    out,
    wqx_v, wox_v, wqy_v, woy_v, wup_v, wdn_v,
    wqx_t, wox_t, wqy_t, woy_t, wup_t,
    gx_t, gy_t, gm_t, gain_v,
    raw_t, raw_c, tokr, cotr, xl, cl, s1r, yl, g1r, g1x, gtx,
    xt, s1t, s2t, g2t, ct, ga, qkvx, qkvy, mixx, mixy, nrm, gmx, gqkv, gpre, ex, ey, ix, iy, sc, dsb, dlt,
    rsem_raw, wsem, ssem, rsem,
):
    gx = lax.axis_index("gx")
    gy = lax.axis_index("gy")
    gyo = lax.rem(gy + 8, 16)
    x_me = gx * 16 + gy
    y_me = gyo * 16 + gx
    X, zh = gx // 4, lax.rem(gx, 4)
    zl, Yc = gy // 8, lax.rem(gy, 8)
    z = zh * 2 + zl

    barrier = pltpu.get_barrier_semaphore()

    def loop(lo, hi, body):
        def step(i, carry):
            body(i)
            return carry

        lax.fori_loop(lo, hi, step, 0)

    row_peers = [
        lax.rem(X + dx, 4) * 4 + lax.rem(zh + zl + dz, 4) for dz in (1, 2, 3, 0) for dx in (2, 1, 3, 0)
    ]
    near = [
        lax.rem(Yc // 2 + dy, 4) * 2 + lax.rem(Yc + dc, 2) for dy in (2, 1, 3, 0) for dc in (1, 0)
    ]
    gy_peers = [lax.rem(zl + dl, 2) * 8 + q for dl in (1, 0) for q in near]

    for q in row_peers:
        pl.semaphore_signal(barrier, inc=1, device_id=(q, gyo), device_id_type=MESH)
    for q in gy_peers[:-1]:
        pl.semaphore_signal(barrier, inc=1, device_id=(gx, q), device_id_type=MESH)

    raws = [
        pltpu.make_async_copy(tok, raw_t, rsem_raw.at[0]),
        pltpu.make_async_copy(cot, raw_c, rsem_raw.at[1]),
        pltpu.make_async_copy(gain_x, gain_v.at[0], rsem_raw.at[2]),
        pltpu.make_async_copy(gain_y, gain_v.at[1], rsem_raw.at[3]),
        pltpu.make_async_copy(gain_m, gain_v.at[2], rsem_raw.at[4]),
    ]
    weights = (
        (wqx, wqx_v), (wox, wox_v), (wqy, wqy_v), (woy, woy_v), (wup, wup_v), (wdn, wdn_v)
    )
    loads = [pltpu.make_async_copy(s, d, wsem.at[i]) for i, (s, d) in enumerate(weights)]
    for load in raws + loads:
        load.start()

    def put(src, dst, device, k):
        pltpu.make_async_remote_copy(
            src_ref=src, dst_ref=dst, send_sem=ssem.at[k], recv_sem=rsem.at[k],
            device_id=device, device_id_type=MESH,
        ).start()

    def keep(src, dst, k):
        pltpu.make_async_copy(src, dst, rsem.at[k]).start()

    def arrived(k):
        pltpu.make_async_copy(yl.at[0], yl.at[0], rsem.at[k]).wait()

    def sent(k, tokens):
        part = yl.at[0, pl.ds(0, tokens)]
        pltpu.make_async_copy(part, part, ssem.at[k]).wait()

    def send_tok(c):
        for q in row_peers:
            put(tokr.at[c, q], xl.at[c, gx], (q, gyo), TOK + c)

    def send_cot(c):
        dst = cl.at[c, gy]
        keep(cotr.at[c, gy], dst, COT + c)
        for q in gy_peers[:-1]:
            put(cotr.at[c, q], dst, (gx, q), COT + c)

    def send_out(c):
        for q in row_peers:
            put(gtx.at[c, q], out.at[gx, c], (q, gyo), OUT + c)

    def outward(k, half):
        return half + jnp.where(k % 2 == 0, k // 2, -((k + 1) // 2))

    def send_all(src, dst, row, me, k, c):
        keep(src.at[c, row(gx, gy)], dst.at[c, me], k + c)

        def body(i, last=0):
            zz = lax.rem(z + outward(i // 4, 4), 8)
            a = lax.rem(X + outward(i % 4, 2), 4) * 4 + zz // 2
            b = (zz % 2) * 8
            for q in near[: 8 - last]:
                put(src.at[c, row(a, b + q)], dst.at[c, me], (a, b + q), k + c)

        loop(0, 31, body)
        body(31, 1)

    def send_xy(c):
        send_all(s1r, yl, lambda a, b: a * 16 + b, y_me, XY, c)

    def send_yx(c):
        send_all(g1r, g1x, lambda a, b: lax.rem(b + 8, 16) * 16 + a, x_me, YX, c)

    def split(raw, dst, swap):
        r = lax.broadcasted_iota(jnp.int32, (N, D), 0)
        s = lax.broadcasted_iota(jnp.int32, (N, D), 1)
        at = (r % 16) * 16 + r // 16 if swap else r
        whole = raw[...].reshape(D, D)
        for c in range(2):
            pick = jnp.where(s == at * 2 + c, 1.0, 0.0).astype(BF)
            dst[c] = nn(pick, whole).astype(BF).reshape(16, 16, D)

    def flip(src, dst, cols):
        def body(i):
            s = pl.multiple_of(i * 256, 256)
            dst[pl.ds(s, 256), :] = jnp.transpose(src[:, pl.ds(s, 256)])

        loop(0, cols // 256, body)

    raws[0].wait()
    split(raw_t, tokr, True)
    raws[1].wait()
    split(raw_c, cotr, False)
    for i, gt in enumerate((gx_t, gy_t, gm_t)):
        raws[2 + i].wait()
        col = jnp.transpose(jnp.broadcast_to(gain_v[i], (128, D)))
        gt[:, :128] = col
        gt[:, 128:] = col
    loads[0].wait()
    flip(wqx_v, wqx_t, 1536)
    loads[1].wait()
    flip(wox_v, wox_t, D)

    pl.semaphore_wait(barrier, 31)
    send_tok(0)
    send_cot(0)
    send_tok(1)

    loads[2].wait()
    flip(wqy_v, wqy_t, 1536)
    loads[3].wait()
    flip(woy_v, woy_t, D)
    loads[4].wait()
    flip(wup_v, wup_t, FF)
    loads[5].wait()

    def forward(src_t, gain_t, wq_t, wo_t, qkv, es, invs, mix, dst_t):
        xhat, _ = norm_parts(src_t[...].astype(F32))
        nrm[...] = (xhat * gain_t[...]).astype(BF)
        qkv[...] = nn(wq_t[...], nrm[...]).astype(BF)
        for h in range(HEADS):
            o = h * HD
            sc[h] = tn(qkv[o + D : o + D + HD, :], qkv[o : o + HD, :] * 0.125)
        for h in range(HEADS):
            for t in (0, 128):
                s = sc[h, :, t : t + 128]
                e = jnp.exp(s - jnp.max(s, 0, keepdims=True))
                invs[h, :, t : t + 128] = 1.0 / jnp.sum(e, 0, keepdims=True)
                es[h, :, t : t + 128] = e.astype(BF)
        for h in range(HEADS):
            o = h * HD
            v = qkv[o + 2 * D : o + 2 * D + HD, :]
            mix[o : o + HD, :] = (nn(v, es[h]) * invs[h]).astype(BF)
        dst_t[...] = (src_t[...].astype(F32) + nn(wo_t[...], mix[...])).astype(BF)

    def heads_back(qkv, es, invs, mix, grad_t, wo):
        gmx[...] = nn(wo[...], grad_t[...]).astype(BF)
        for h in range(HEADS):
            o = h * HD
            gi = gmx[o : o + HD, :].astype(F32) * invs[h]
            dlt[h] = jnp.sum(gi * mix[o : o + HD, :].astype(F32), 0, keepdims=True)
            gi = gi.astype(BF)
            gmx[o : o + HD, :] = gi
            sc[h] = tn(qkv[o + 2 * D : o + 2 * D + HD, :], gi)
        for h in range(HEADS):
            o = h * HD
            gqkv[o + 2 * D : o + 2 * D + HD, :] = nt(gmx[o : o + HD, :], es[h]).astype(BF)
        for h in range(HEADS):
            dsb[h] = (es[h].astype(F32) * (sc[h] - dlt[h])).astype(BF)
        for h in range(HEADS):
            o = h * HD
            gqkv[o : o + HD, :] = (nn(qkv[o + D : o + D + HD, :], dsb[h]) * 0.125).astype(BF)
            gqkv[o + D : o + D + HD, :] = (nt(qkv[o : o + HD, :], dsb[h]) * 0.125).astype(BF)

    def finish_back(src_t, grad_t, gain_t, wq):
        e = nn(wq[...], gqkv[...])
        return grad_t[...].astype(F32) + norm_back(src_t[...].astype(F32), gain_t[...], e)

    def x_fwd(c):
        arrived(TOK + c)
        xt[c] = jnp.transpose(xl[c].reshape(N, D))
        forward(xt.at[c], gx_t, wqx_t, wox_t, qkvx.at[c], ex.at[c], ix.at[c], mixx.at[c], s2t)
        s1r[c] = jnp.transpose(s2t[...]).reshape(N, 4, 128)
        send_xy(c)

    def y_act(c):
        arrived(COT + c)
        ct[c] = jnp.transpose(cl[c].reshape(N, D))
        ga[c] = nn(wdn_v[...], ct[c]).astype(BF)

    def y_fwd(c):
        arrived(XY + c)
        s1t[...] = jnp.transpose(yl[c].reshape(N, D))
        forward(s1t, gy_t, wqy_t, woy_t, qkvy, ey, iy, mixy, s2t)

    def y_mlp(c):
        xhat, _ = norm_parts(s2t[...].astype(F32))
        nrm[...] = (xhat * gm_t[...]).astype(BF)
        gpre[...] = (
            ga[c].astype(F32) * gelu_slope(nn(wup_t[...], nrm[...]))
        ).astype(BF)
        e = nn(wup_v[...], gpre[...])
        g2t[...] = (
            ct[c].astype(F32) + norm_back(s2t[...].astype(F32), gm_t[...], e)
        ).astype(BF)

    def y_bwd(c):
        heads_back(qkvy, ey, iy, mixy, g2t, woy_v)
        g = finish_back(s1t, g2t, gy_t, wqy_v).astype(BF)
        g1r[c] = jnp.transpose(g).reshape(N, 4, 128)
        send_yx(c)

    def x_bwd(c):
        arrived(YX + c)
        g2t[...] = jnp.transpose(g1x[c].reshape(N, D))
        heads_back(qkvx.at[c], ex.at[c], ix.at[c], mixx.at[c], g2t, wox_v)
        g = finish_back(xt.at[c], g2t, gx_t, wqx_v).astype(BF)
        gtx[c] = jnp.transpose(g).reshape(16, 16, D)
        send_out(c)

    x_fwd(0)
    x_fwd(1)
    send_cot(1)
    y_act(0)
    y_fwd(0)
    y_mlp(0)
    y_bwd(0)
    y_fwd(1)
    y_act(1)
    y_mlp(1)
    y_bwd(1)
    x_bwd(0)
    x_bwd(1)

    for c in range(2):
        arrived(OUT + c)
        sent(TOK + c, 256)
        sent(COT + c, 240)
        sent(XY + c, 255)
        sent(YX + c, 255)
        sent(OUT + c, 256)


def local(
    tokens, cotangent, gain_x, w_qkv_x, w_out_x, gain_y, w_qkv_y, w_out_y, gain_mlp, w_up, w_down
):
    any_spec = pl.BlockSpec(memory_space=pl.ANY)
    V = pltpu.VMEM
    scratch = [
        V((D, 1536), BF), V((D, D), BF), V((D, 1536), BF), V((D, D), BF), V((D, FF), BF),
        V((FF, D), BF),
        V((1536, D), BF), V((D, D), BF), V((1536, D), BF), V((D, D), BF), V((FF, D), BF),
        V((D, N), F32), V((D, N), F32), V((D, N), F32), V((3, 1, D), F32),
        V((16, 16, 2, D), BF), V((16, 16, 2, D), BF),
        V((2, 16, 16, D), BF), V((2, 16, 16, D), BF),
        V((2, 16, 16, D), BF), V((2, 16, 16, D), BF),
        V((2, N, 4, 128), BF), V((2, N, 4, 128), BF),
        V((2, N, 4, 128), BF), V((2, N, 4, 128), BF),
        V((2, 16, 16, D), BF),
        V((2, D, N), BF),
        V((D, N), BF), V((D, N), BF), V((D, N), BF),
        V((2, D, N), BF), V((2, FF, N), BF),
        V((2, 1536, N), BF), V((1536, N), BF),
        V((2, D, N), BF), V((D, N), BF), V((D, N), BF), V((D, N), BF),
        V((1536, N), BF), V((FF, N), BF),
        V((2, HEADS, N, N), BF), V((HEADS, N, N), BF),
        V((2, HEADS, 1, N), F32), V((HEADS, 1, N), F32),
        V((HEADS, N, N), F32), V((HEADS, N, N), BF), V((HEADS, 1, N), F32),
        pltpu.SemaphoreType.DMA((5,)),
        pltpu.SemaphoreType.DMA((6,)),
        pltpu.SemaphoreType.DMA((N_EX,)),
        pltpu.SemaphoreType.DMA((N_EX,)),
    ]
    res = pl.pallas_call(
        kernel,
        out_shape=jax.ShapeDtypeStruct((16, 2, 16, D), BF),
        in_specs=[any_spec] * 11,
        out_specs=any_spec,
        scratch_shapes=scratch,
        compiler_params=pltpu.CompilerParams(
            collective_id=0, has_side_effects=True, vmem_limit_bytes=60 * 1024 * 1024
        ),
        name="axial_grad",
    )(
        tokens, cotangent, gain_x.reshape(1, D), w_qkv_x, w_out_x, gain_y.reshape(1, D), w_qkv_y,
        w_out_y, gain_mlp.reshape(1, D), w_up, w_down,
    )
    return jnp.transpose(res, (2, 0, 1, 3))


def solution(mesh):
    in_specs = (P("gx", "gy", None, None), P("gx", "gy", None, None)) + (P(),) * 9
    out_specs = P("gx", "gy", None, None)
    return jax.shard_map(local, mesh=mesh, in_specs=in_specs, out_specs=out_specs, check_vma=False)
```
